1024 devices in a mesh: seq: 64 (over y, z_lo, core), chan: 16 (over x, z_hi).
Axes of the slice: x: 8, y: 8, z: 8 (z_hi: 2, z_lo: 4; z = z_hi * 4 + z_lo), core: 2. Of those that a mesh axis runs over, the one named last changes fastest.
Arguments:
- tokens: bfloat16 [16384, 2048], P('seq', 'chan'), may hold values from -6 to 6
- in_weight: bfloat16 [3, 2048, 2048], P(None, None, 'chan'), may hold values from -0.125 to 0.125
- out_weight: bfloat16 [2048, 2048], P(None, 'chan'), may hold values from -0.125 to 0.125
- decay_rates: float32 [16, 2048], P(None, 'chan'), may hold values from 6.1035156e-05 to 0.03
- residues: float32 [16, 2048], P(None, 'chan'), may hold values from -1.8 to 1.8
- skip_gain: float32 [2048], P('chan'), may hold values from -5 to 5
Outputs:
- block_out: bfloat16 [16384, 2048], P('seq', 'chan')
The draws below stay inside these ranges and needn't reach their ends.
All inputs are finite; a program needn't handle non-finite values.
Results may differ from the reference program's by a relative error of at most 0.013.
Values may be sent and summed in bfloat16 or wider, within the bound.
No kernel may reach another device: no remote copies, remote signals or barrier semaphores. Data moves between devices by JAX's collectives and lax.ppermute only.
A program may use at most 32 MiB of HBM per device.

```python
import math
import jax
import jax.numpy as jnp
from jax import lax

CH_DEV = 128
MODES = 16
CHANNELS = 2048
LENGTH = 16384


def levels(own_key, dims, cuts, least, top_value):
    def one(position, parts):
        draws = jax.random.uniform(jax.random.fold_in(jax.random.fold_in(own_key, 6), position), (parts,), jnp.float32, least / len(cuts), top_value / len(cuts))
        return jnp.repeat(jnp.exp(draws), dims[position] // parts).reshape((-1,) + (1,) * (len(dims) - position - 1))

    loudness = one(*cuts[0])
    for cut in cuts[1:]:
        loudness = loudness * one(*cut)
    return loudness


def noise(rng, shape, spread, bound, pieces=(), held_as=jnp.bfloat16):
    loudness = levels(rng, shape, pieces, -0.22, 0.18) if pieces else 1.0
    entries = jax.random.normal(rng, shape, jnp.float32) * spread * loudness
    return jnp.minimum(jnp.maximum(entries, -bound), bound).astype(held_as)


def setup_inputs(seed: int = 0) -> dict:
    arg_keys = jax.random.split(jax.random.key(seed), 7)
    return {
        "tokens": noise(arg_keys[0], (LENGTH, CHANNELS), 1.0, 6.0, ((0, 64), (1, 16))),
        "in_weight": noise(arg_keys[1], (3, CHANNELS, CHANNELS), CHANNELS ** -0.5, 0.125, ((2, 16),)),
        "out_weight": noise(arg_keys[2], (CHANNELS, CHANNELS), CHANNELS ** -0.5, 0.125, ((1, 16),)),
        "decay_rates": jnp.clip(jnp.exp(math.log(0.03) - 6.1975026 * jax.random.uniform(arg_keys[3], (MODES, CHANNELS), jnp.float32) ** levels(arg_keys[3], (MODES, CHANNELS), ((1, 16),), -0.2, 0.2)), 6.103515625e-05, 0.03),
        "residues": noise(arg_keys[4], (MODES, CHANNELS), 0.3, 1.8, ((1, 16),), jnp.float32),
        "skip_gain": noise(arg_keys[5], (CHANNELS,), 1.0, 5.0, ((0, 16),), jnp.float32),
    }


def reference(tokens, in_weight, out_weight, decay_rates, residues, skip_gain):
    projected = jnp.stack([jnp.dot(tokens, in_weight[index], preferred_element_type=jnp.float32) for index in range(3)]).astype(jnp.bfloat16)
    product = projected[1].astype(jnp.float32) * projected[2].astype(jnp.float32)
    blocks = CHANNELS // CH_DEV
    positions = jnp.arange(LENGTH, dtype=jnp.float32)

    def one_block(block_args):
        signal, rates, weights = block_args

        def add_mode(mode_index, impulse):
            rate = rates[mode_index]
            return impulse + weights[mode_index] * jnp.sqrt(2.0 * rate) * jnp.exp(-rate * positions[:, None])
        impulse = lax.fori_loop(0, MODES, add_mode, jnp.zeros((LENGTH, CH_DEV), jnp.float32))
        spectrum = jnp.fft.rfft(signal, n=2 * LENGTH, axis=0) * jnp.fft.rfft(impulse, n=2 * LENGTH, axis=0)
        return jnp.fft.irfft(spectrum, n=2 * LENGTH, axis=0)[:LENGTH].astype(jnp.float32)
    stacked = product.reshape(LENGTH, blocks, CH_DEV).transpose(1, 0, 2)
    rate_blocks = decay_rates.reshape(MODES, blocks, CH_DEV).transpose(1, 0, 2)
    weight_blocks = residues.reshape(MODES, blocks, CH_DEV).transpose(1, 0, 2)
    convolved = lax.map(one_block, (stacked, rate_blocks, weight_blocks)).transpose(1, 0, 2).reshape(LENGTH, CHANNELS)
    mixed = (projected[0].astype(jnp.float32) * (convolved + skip_gain[None, :] * product)).astype(jnp.bfloat16)
    return jnp.dot(mixed, out_weight, preferred_element_type=jnp.float32).astype(jnp.bfloat16)
```

```python
import functools

import jax
import jax.numpy as jnp
from jax import lax
from jax.experimental import pallas as pl
from jax.experimental.pallas import tpu as pltpu
from jax.sharding import PartitionSpec as P


F32 = jnp.float32
BF16 = jnp.bfloat16
VMEM = pltpu.VMEM
SMEM = pltpu.SMEM
STEP = 16
LANE_TILE = 8


def table_kernel(decay_ref, residue_ref, skip_ref, power_ref, impulse_ref, chunk_ref, small_ref):
    rate = decay_ref[...]
    modes, chans = rate.shape
    chunks = chunk_ref.shape[0] // modes
    gain = residue_ref[...] * jnp.sqrt(2.0 * rate)
    for k in range(STEP + 1):
        power = jnp.exp(rate * (-float(k)))
        for m in range(modes):
            power_ref[k * modes + m] = jnp.broadcast_to(power[m : m + 1, :], (LANE_TILE, chans))
        if k < STEP:
            tap = jnp.sum(gain * power, axis=0, keepdims=True)
            if k == 0:
                tap = tap + skip_ref[...]
            impulse_ref[k] = jnp.broadcast_to(tap, (LANE_TILE, chans))
    for i in range(chunks):
        chunk_ref[pl.ds(i * modes, modes), :] = jnp.exp(rate * (-float(STEP * i)))
    small_ref[0] = gain
    small_ref[1] = jnp.exp(rate * (-float(STEP)))


def tables(decay, residue, skip, rows):
    modes, chans = decay.shape
    chunks = rows // STEP
    return pl.pallas_call(
        table_kernel,
        out_shape=(
            jax.ShapeDtypeStruct(((STEP + 1) * modes, LANE_TILE, chans), F32),
            jax.ShapeDtypeStruct((STEP, LANE_TILE, chans), F32),
            jax.ShapeDtypeStruct((chunks * modes, chans), F32),
            jax.ShapeDtypeStruct((2, modes, chans), F32),
        ),
        cost_estimate=pl.CostEstimate(flops=2_000_000, bytes_accessed=1_500_000, transcendentals=70_000),
    )(decay, residue, skip)


def gathered_dot(half, near_ref, far_ref, weights):
    hops, rows, chans = near_ref.shape
    total = None
    for hop in range(hops):
        left = jnp.concatenate([near_ref[hop], far_ref[hop]], axis=1)
        near_row = pl.multiple_of((2 * hop + half) * chans, chans)
        far_row = pl.multiple_of((2 * hop + 1 - half) * chans, chans)
        right = jnp.concatenate([weights(near_row, chans), weights(far_row, chans)], axis=0)
        part = jnp.dot(left, right, preferred_element_type=F32)
        total = part if total is None else total + part
    return total


def project_kernel(
    half_ref, near_ref, far_ref, weight_ref, power_ref, small_ref,
    query_ref, product_ref, carry_ref, state_ref, ends,
):
    half = half_ref[0]
    chans = near_ref.shape[2]
    modes = small_ref.shape[1]
    chunks = product_ref.shape[0] // STEP

    def one(index):
        return lambda row, count: weight_ref[index, pl.ds(row, count), :]

    def pair(row, count):
        return jnp.concatenate([one(1)(row, count), one(2)(row, count)], axis=1)

    both = gathered_dot(half, near_ref, far_ref, pair)
    keys = both[:, :chans].astype(BF16).astype(F32)
    values = both[:, chans:].astype(BF16).astype(F32)
    product_ref[...] = keys * values
    query_ref[...] = gathered_dot(half, near_ref, far_ref, one(0)).astype(BF16).astype(F32)

    signal = [product_ref[pl.ds(j, chunks, stride=STEP), :] for j in range(STEP)]
    parts = chunks // LANE_TILE
    for m in range(modes):
        sums = [None] * parts
        for j in range(STEP):
            power = power_ref[(STEP - 1 - j) * modes + m]
            for h in range(parts):
                term = power * signal[j][h * LANE_TILE : (h + 1) * LANE_TILE, :]
                sums[h] = term if sums[h] is None else sums[h] + term
        ends[pl.ds(m, chunks, stride=modes), :] = jnp.concatenate(sums, axis=0)
    gain = small_ref[0]
    decay = small_ref[1]
    state = jnp.zeros((modes, chans), F32)
    for i in range(chunks):
        carry_ref[pl.ds(i * modes, modes), :] = state
        state = decay * state + gain * ends[pl.ds(i * modes, modes), :]
    state_ref[...] = state


def project(half, near, far, weight, power, small):
    rows, chans = near.shape[1:]
    modes = small.shape[1]
    chunks = rows // STEP
    return pl.pallas_call(
        project_kernel,
        in_specs=[pl.BlockSpec(memory_space=SMEM)] + [pl.BlockSpec(memory_space=VMEM)] * 5,
        out_shape=(
            jax.ShapeDtypeStruct((rows, chans), F32),
            jax.ShapeDtypeStruct((rows, chans), F32),
            jax.ShapeDtypeStruct((chunks * modes, chans), F32),
            jax.ShapeDtypeStruct((modes, chans), F32),
        ),
        scratch_shapes=[VMEM((chunks * modes, chans), F32)],
    )(half, near, far, weight, power, small)


def block_total_kernel(span, decay_ref, states_ref, total_ref):
    rate = decay_ref[...]
    decay = jnp.exp(rate * (-float(span)))
    total = states_ref[0]
    for i in range(1, states_ref.shape[0]):
        total = decay * total + states_ref[i]
    total_ref[...] = total


def block_total(decay, states, span):
    return pl.pallas_call(
        functools.partial(block_total_kernel, span),
        out_shape=jax.ShapeDtypeStruct(states.shape[1:], F32),
    )(decay, states)


def prefix(count, place, states_ref, decay):
    total = jnp.zeros(states_ref.shape[1:], F32)
    for i in range(count - 1):
        total = jnp.where(i < place, decay * total + states_ref[i], total)
    return total


def combine_kernel(
    span, place_ref, decay_ref, inner_ref, outer_ref, query_ref, product_ref, carry_ref,
    power_ref, impulse_ref, chunk_ref, mixed_ref, states, result,
):
    inner = inner_ref.shape[0]
    outer = outer_ref.shape[0]
    modes, chans = decay_ref.shape
    rows = product_ref.shape[0]
    chunks = rows // STEP
    parts = chunks // LANE_TILE
    inner_place = place_ref[0]
    outer_place = place_ref[1]
    rate = decay_ref[...]
    near = prefix(inner, inner_place, inner_ref, jnp.exp(rate * (-float(span))))
    far = prefix(outer, outer_place, outer_ref, jnp.exp(rate * (-float(span * inner))))
    reach = inner_place.astype(F32) * float(span)
    start = near + jnp.exp(-rate * reach) * far
    for i in range(chunks):
        spot = pl.ds(i * modes, modes)
        states[spot, :] = carry_ref[spot, :] + chunk_ref[spot, :] * start
    state = [states[pl.ds(m, chunks, stride=modes), :] for m in range(modes)]
    for j in range(STEP):
        sums = [None] * parts
        for m in range(modes):
            power = power_ref[(j + 1) * modes + m]
            for h in range(parts):
                term = power * state[m][h * LANE_TILE : (h + 1) * LANE_TILE, :]
                sums[h] = term if sums[h] is None else sums[h] + term
        result[pl.ds(j, chunks, stride=STEP), :] = jnp.concatenate(sums, axis=0)
    signal = [product_ref[pl.ds(j, chunks, stride=STEP), :] for j in range(STEP)]
    for j in range(STEP):
        spot = pl.ds(j, chunks, stride=STEP)
        sums = [None] * parts
        for k in range(j + 1):
            tap = impulse_ref[k]
            for h in range(parts):
                term = tap * signal[j - k][h * LANE_TILE : (h + 1) * LANE_TILE, :]
                sums[h] = term if sums[h] is None else sums[h] + term
        result[spot, :] = (result[spot, :] + jnp.concatenate(sums, axis=0)) * query_ref[spot, :]
    mixed_ref[...] = result[...].astype(BF16)


def combine(place, decay, inner, outer, query, product, carry, power, impulse, chunk):
    rows, chans = product.shape
    return pl.pallas_call(
        functools.partial(combine_kernel, rows),
        in_specs=[pl.BlockSpec(memory_space=SMEM)] + [pl.BlockSpec(memory_space=VMEM)] * 9,
        out_shape=jax.ShapeDtypeStruct((rows, chans), BF16),
        scratch_shapes=[VMEM(carry.shape, F32), VMEM((rows, chans), F32)],
    )(place, decay, inner, outer, query, product, carry, power, impulse, chunk)


def output_kernel(half_ref, near_ref, far_ref, weight_ref, out_ref):
    out_ref[...] = gathered_dot(
        half_ref[0], near_ref, far_ref, lambda row, count: weight_ref[pl.ds(row, count), :]
    ).astype(BF16)


def output(half, near, far, weight):
    rows, chans = near.shape[1:]
    return pl.pallas_call(
        output_kernel,
        in_specs=[pl.BlockSpec(memory_space=SMEM)] + [pl.BlockSpec(memory_space=VMEM)] * 3,
        out_shape=jax.ShapeDtypeStruct((rows, weight.shape[1]), BF16),
    )(half, near, far, weight)


def gather_channels(block, between=None):
    count = lax.axis_size("chan")
    groups = [list(range(z, count, 2)) for z in range(2)]
    swapped = lax.ppermute(block, "chan", [(c, c ^ 1) for c in range(count)])
    near = lax.all_gather(block, "chan", axis_index_groups=groups)
    swapped, near = lax.optimization_barrier((swapped, near))
    far = lax.all_gather(swapped, "chan", axis_index_groups=groups)
    return near, far


def exchange(block, groups):
    copies = jnp.broadcast_to(block[None], (len(groups[0]),) + block.shape)
    return lax.all_to_all(copies, "seq", 0, 0, tiled=True, axis_index_groups=groups)


def on_device(tokens, in_weight, out_weight, decay_rates, residues, skip_gain):
    seq_count = lax.axis_size("seq")
    seq_place = lax.axis_index("seq")
    half = (lax.axis_index("chan") % 2).astype(jnp.int32).reshape(1)
    rows, chans = tokens.shape
    inner = 8
    outer = seq_count // inner
    power, impulse, chunk, small = tables(decay_rates, residues, skip_gain[None, :], rows)
    near, far = gather_channels(tokens)
    query, product, carry, state = project(half, near, far, in_weight, power, small)
    inner_groups = [[o * inner + i for i in range(inner)] for o in range(outer)]
    outer_groups = [[o * inner + i for o in range(outer)] for i in range(inner)]
    inner_states = exchange(state, inner_groups)
    total = block_total(decay_rates, inner_states, rows)
    outer_states = exchange(total, outer_groups)
    place = jnp.stack([seq_place % inner, seq_place // inner]).astype(jnp.int32)
    mixed = combine(
        place, decay_rates, inner_states, outer_states, query, product, carry, power, impulse, chunk
    )
    near, far = gather_channels(mixed)
    return output(half, near, far, out_weight)


def solution(mesh):
    return jax.shard_map(
        on_device,
        mesh=mesh,
        in_specs=(
            P("seq", "chan"),
            P(None, None, "chan"),
            P(None, "chan"),
            P(None, "chan"),
            P(None, "chan"),
            P("chan"),
        ),
        out_specs=P("seq", "chan"),
        check_vma=False,
    )
```

```python
import functools

import jax
import jax.numpy as jnp
from jax import lax
from jax.experimental import pallas as pl
from jax.experimental.pallas import tpu as pltpu
from jax.sharding import PartitionSpec as P


F32 = jnp.float32
BF16 = jnp.bfloat16
VMEM = pltpu.VMEM
SMEM = pltpu.SMEM
STEP = 16
LANE_TILE = 8
PARAMS = pltpu.CompilerParams(vmem_limit_bytes=12 * 1024 * 1024)


def table_kernel(decay_ref, residue_ref, skip_ref, power_ref, impulse_ref, chunk_ref, small_ref):
    rate = decay_ref[...]
    modes, chans = rate.shape
    chunks = chunk_ref.shape[0] // modes
    gain = residue_ref[...] * jnp.sqrt(2.0 * rate)
    for k in range(STEP + 1):
        power = jnp.exp(rate * (-float(k)))
        for m in range(modes):
            power_ref[k * modes + m] = jnp.broadcast_to(power[m : m + 1, :], (LANE_TILE, chans))
        if k < STEP:
            tap = jnp.sum(gain * power, axis=0, keepdims=True)
            if k == 0:
                tap = tap + skip_ref[...]
            impulse_ref[k] = jnp.broadcast_to(tap, (LANE_TILE, chans))
    for i in range(chunks):
        chunk_ref[pl.ds(i * modes, modes), :] = jnp.exp(rate * (-float(STEP * i)))
    small_ref[0] = gain
    small_ref[1] = jnp.exp(rate * (-float(STEP)))


def tables(decay, residue, skip, rows):
    modes, chans = decay.shape
    chunks = rows // STEP
    return pl.pallas_call(
        table_kernel,
        out_shape=(
            jax.ShapeDtypeStruct(((STEP + 1) * modes, LANE_TILE, chans), F32),
            jax.ShapeDtypeStruct((STEP, LANE_TILE, chans), F32),
            jax.ShapeDtypeStruct((chunks * modes, chans), F32),
            jax.ShapeDtypeStruct((2, modes, chans), F32),
        ),
        cost_estimate=pl.CostEstimate(flops=2_000_000, bytes_accessed=1_500_000, transcendentals=70_000),
        compiler_params=PARAMS,
    )(decay, residue, skip)


def half_dot(half, block_ref, weights):
    hops, rows, chans = block_ref.shape
    pack = 2 if hops % 2 == 0 else 1
    total = None
    for hop in range(0, hops, pack):
        left = jnp.concatenate([block_ref[hop + i] for i in range(pack)], axis=1)
        spots = [pl.multiple_of((2 * (hop + i) + half) * chans, chans) for i in range(pack)]
        right = jnp.concatenate([weights(pl.ds(spot, chans)) for spot in spots], axis=0)
        part = jnp.dot(left, right, preferred_element_type=F32)
        total = part if total is None else total + part
    return total


def keys_values(weight_ref):
    return lambda spot: jnp.concatenate([weight_ref[1, spot, :], weight_ref[2, spot, :]], axis=1)


def near_kernel(weight_ref, near_ref, both_ref, query_ref):
    half = lax.axis_index("chan") % 2
    both_ref[...] = half_dot(half, near_ref, keys_values(weight_ref))
    query_ref[...] = half_dot(half, near_ref, lambda spot: weight_ref[0, spot, :])


def near_project(weight, near):
    rows, chans = near.shape[1:]
    return pl.pallas_call(
        near_kernel,
        out_shape=(
            jax.ShapeDtypeStruct((rows, 2 * chans), F32),
            jax.ShapeDtypeStruct((rows, chans), F32),
        ),
        compiler_params=PARAMS,
        cost_estimate=pl.CostEstimate(flops=200_000_000, bytes_accessed=1_700_000, transcendentals=0),
    )(weight, near)


def project_kernel(
    far_ref, near_both_ref, near_query_ref, weight_ref, power_ref, small_ref,
    query_ref, product_ref, carry_ref, state_ref, ends,
):
    other = 1 - lax.axis_index("chan") % 2
    rows, chans = product_ref.shape
    modes = small_ref.shape[1]
    chunks = rows // STEP

    both = near_both_ref[...] + half_dot(other, far_ref, keys_values(weight_ref))
    keys = both[:, :chans].astype(BF16).astype(F32)
    values = both[:, chans:].astype(BF16).astype(F32)
    product_ref[...] = keys * values
    query = near_query_ref[...] + half_dot(other, far_ref, lambda spot: weight_ref[0, spot, :])
    query_ref[...] = query.astype(BF16).astype(F32)

    signal = [product_ref[pl.ds(j, chunks, stride=STEP), :] for j in range(STEP)]
    parts = chunks // LANE_TILE
    for m in range(modes):
        sums = [None] * parts
        for j in range(STEP):
            power = power_ref[(STEP - 1 - j) * modes + m]
            for h in range(parts):
                term = power * signal[j][h * LANE_TILE : (h + 1) * LANE_TILE, :]
                sums[h] = term if sums[h] is None else sums[h] + term
        ends[pl.ds(m, chunks, stride=modes), :] = jnp.concatenate(sums, axis=0)
    gain = small_ref[0]
    decay = small_ref[1]
    state = jnp.zeros((modes, chans), F32)
    for i in range(chunks):
        carry_ref[pl.ds(i * modes, modes), :] = state
        state = decay * state + gain * ends[pl.ds(i * modes, modes), :]
    for i in range(state_ref.shape[0]):
        state_ref[i] = state


def project(far, near_both, near_query, weight, power, small, copies):
    rows, chans = far.shape[1:]
    modes = small.shape[1]
    chunks = rows // STEP
    return pl.pallas_call(
        project_kernel,
        out_shape=(
            jax.ShapeDtypeStruct((rows, chans), F32),
            jax.ShapeDtypeStruct((rows, chans), F32),
            jax.ShapeDtypeStruct((chunks * modes, chans), F32),
            jax.ShapeDtypeStruct((copies, modes, chans), F32),
        ),
        scratch_shapes=[VMEM((chunks * modes, chans), F32)],
        compiler_params=PARAMS,
        cost_estimate=pl.CostEstimate(flops=210_000_000, bytes_accessed=3_000_000, transcendentals=0),
    )(far, near_both, near_query, weight, power, small)


def block_total_kernel(span, decay_ref, states_ref, total_ref):
    rate = decay_ref[...]
    decay = jnp.exp(rate * (-float(span)))
    total = states_ref[0]
    for i in range(1, states_ref.shape[0]):
        total = decay * total + states_ref[i]
    for i in range(total_ref.shape[0]):
        total_ref[i] = total


def block_total(decay, states, span, copies):
    return pl.pallas_call(
        functools.partial(block_total_kernel, span),
        out_shape=jax.ShapeDtypeStruct((copies,) + states.shape[1:], F32),
        compiler_params=PARAMS,
    )(decay, states)


def prefix(count, place, states_ref, decay):
    total = jnp.zeros(states_ref.shape[1:], F32)
    for i in range(count - 1):
        total = jnp.where(i < place, decay * total + states_ref[i], total)
    return total


def combine_kernel(
    span, decay_ref, inner_ref, outer_ref, query_ref, product_ref, carry_ref,
    power_ref, impulse_ref, chunk_ref, mixed_ref, copies_ref, states, result,
):
    inner = inner_ref.shape[0]
    outer = outer_ref.shape[0]
    modes, chans = decay_ref.shape
    rows = product_ref.shape[0]
    chunks = rows // STEP
    parts = chunks // LANE_TILE
    place = lax.axis_index("seq")
    inner_place = place % inner
    outer_place = place // inner
    rate = decay_ref[...]
    near = prefix(inner, inner_place, inner_ref, jnp.exp(rate * (-float(span))))
    far = prefix(outer, outer_place, outer_ref, jnp.exp(rate * (-float(span * inner))))
    reach = inner_place.astype(F32) * float(span)
    start = near + jnp.exp(-rate * reach) * far
    for i in range(chunks):
        spot = pl.ds(i * modes, modes)
        states[spot, :] = carry_ref[spot, :] + chunk_ref[spot, :] * start
    state = [states[pl.ds(m, chunks, stride=modes), :] for m in range(modes)]
    for j in range(STEP):
        sums = [None] * parts
        for m in range(modes):
            power = power_ref[(j + 1) * modes + m]
            for h in range(parts):
                term = power * state[m][h * LANE_TILE : (h + 1) * LANE_TILE, :]
                sums[h] = term if sums[h] is None else sums[h] + term
        result[pl.ds(j, chunks, stride=STEP), :] = jnp.concatenate(sums, axis=0)
    signal = [product_ref[pl.ds(j, chunks, stride=STEP), :] for j in range(STEP)]
    for j in range(STEP):
        spot = pl.ds(j, chunks, stride=STEP)
        sums = [None] * parts
        for k in range(j + 1):
            tap = impulse_ref[k]
            for h in range(parts):
                term = tap * signal[j - k][h * LANE_TILE : (h + 1) * LANE_TILE, :]
                sums[h] = term if sums[h] is None else sums[h] + term
        result[spot, :] = (result[spot, :] + jnp.concatenate(sums, axis=0)) * query_ref[spot, :]
    mixed = result[...].astype(BF16)
    mixed_ref[...] = mixed
    for i in range(copies_ref.shape[0]):
        copies_ref[i] = mixed


def combine(decay, inner, outer, query, product, carry, power, impulse, chunk, copies):
    rows, chans = product.shape
    return pl.pallas_call(
        functools.partial(combine_kernel, rows),
        out_shape=(
            jax.ShapeDtypeStruct((rows, chans), BF16),
            jax.ShapeDtypeStruct((copies, rows, chans), BF16),
        ),
        scratch_shapes=[VMEM(carry.shape, F32), VMEM((rows, chans), F32)],
        compiler_params=PARAMS,
        cost_estimate=pl.CostEstimate(flops=3_000_000, bytes_accessed=3_000_000, transcendentals=10_000),
    )(decay, inner, outer, query, product, carry, power, impulse, chunk)


def near_output_kernel(weight_ref, near_ref, out_ref):
    half = lax.axis_index("chan") % 2
    out_ref[...] = half_dot(half, near_ref, lambda spot: weight_ref[spot, :])


def near_output(weight, near):
    rows = near.shape[1]
    return pl.pallas_call(
        near_output_kernel,
        out_shape=jax.ShapeDtypeStruct((rows, weight.shape[1]), F32),
        compiler_params=PARAMS,
        cost_estimate=pl.CostEstimate(flops=70_000_000, bytes_accessed=1_100_000, transcendentals=0),
    )(weight, near)


def output_kernel(far_ref, partial_ref, weight_ref, out_ref):
    other = 1 - lax.axis_index("chan") % 2
    total = partial_ref[...] + half_dot(other, far_ref, lambda spot: weight_ref[spot, :])
    out_ref[...] = total.astype(BF16)


def output(far, partial, weight):
    rows = far.shape[1]
    return pl.pallas_call(
        output_kernel,
        out_shape=jax.ShapeDtypeStruct((rows, weight.shape[1]), BF16),
        compiler_params=PARAMS,
        cost_estimate=pl.CostEstimate(flops=70_000_000, bytes_accessed=1_100_000, transcendentals=0),
    )(far, partial, weight)


def copied(block, count):
    return jnp.broadcast_to(block[None], (count,) + block.shape)


def exchange(copies, axis, groups):
    return lax.all_to_all(copies, axis, 0, 0, tiled=True, axis_index_groups=groups)


def on_device(tokens, in_weight, out_weight, decay_rates, residues, skip_gain):
    seq_count = lax.axis_size("seq")
    chan_count = lax.axis_size("chan")
    rows, chans = tokens.shape
    inner = 8
    outer = seq_count // inner
    hops = chan_count // 2
    inner_groups = [[o * inner + i for i in range(inner)] for o in range(outer)]
    outer_groups = [[o * inner + i for o in range(outer)] for i in range(inner)]
    row_groups = [list(range(z, chan_count, 2)) for z in range(2)]
    swap = [(c, c ^ 1) for c in range(chan_count)]

    swapped = lax.ppermute(tokens, "chan", swap)
    power, impulse, chunk, small = tables(decay_rates, residues, skip_gain[None, :], rows)
    near = exchange(copied(tokens, hops), "chan", row_groups)
    far = exchange(copied(swapped, hops), "chan", row_groups)
    near_both, near_query = near_project(in_weight, near)
    query, product, carry, states = project(
        far, near_both, near_query, in_weight, power, small, inner
    )
    inner_states = exchange(states, "seq", inner_groups)
    totals = block_total(decay_rates, inner_states, rows, outer)
    outer_states = exchange(totals, "seq", outer_groups)
    mixed, copies = combine(
        decay_rates, inner_states, outer_states, query, product, carry, power, impulse, chunk, hops
    )
    swapped = lax.ppermute(mixed, "chan", swap)
    near = exchange(copies, "chan", row_groups)
    far = exchange(copied(swapped, hops), "chan", row_groups)
    return output(far, near_output(out_weight, near), out_weight)


def solution(mesh):
    return jax.shard_map(
        on_device,
        mesh=mesh,
        in_specs=(
            P("seq", "chan"),
            P(None, None, "chan"),
            P(None, "chan"),
            P(None, "chan"),
            P(None, "chan"),
            P("chan"),
        ),
        out_specs=P("seq", "chan"),
        check_vma=False,
    )
```

```python
import functools

import jax
import jax.numpy as jnp
from jax import lax
from jax.experimental import pallas as pl
from jax.experimental.pallas import tpu as pltpu
from jax.sharding import PartitionSpec as P


F32 = jnp.float32
BF16 = jnp.bfloat16
VMEM = pltpu.VMEM
STEP = 16
LANE_TILE = 8
PARAMS = pltpu.CompilerParams(vmem_limit_bytes=12 * 1024 * 1024)


def table_kernel(decay_ref, residue_ref, skip_ref, power_ref, impulse_ref, chunk_ref, small_ref):
    rate = decay_ref[...]
    modes, chans = rate.shape
    chunks = chunk_ref.shape[0] // modes
    gain = residue_ref[...] * jnp.sqrt(2.0 * rate)
    for k in range(STEP + 1):
        power = jnp.exp(rate * (-float(k)))
        for m in range(modes):
            power_ref[k * modes + m] = jnp.broadcast_to(power[m : m + 1, :], (LANE_TILE, chans))
        if k < STEP:
            tap = jnp.sum(gain * power, axis=0, keepdims=True)
            if k == 0:
                tap = tap + skip_ref[...]
            impulse_ref[k] = jnp.broadcast_to(tap, (LANE_TILE, chans))
    for i in range(chunks):
        chunk_ref[pl.ds(i * modes, modes), :] = jnp.exp(rate * (-float(STEP * i)))
    small_ref[0] = gain
    small_ref[1] = jnp.exp(rate * (-float(STEP)))


def tables(decay, residue, skip, rows):
    modes, chans = decay.shape
    chunks = rows // STEP
    return pl.pallas_call(
        table_kernel,
        out_shape=(
            jax.ShapeDtypeStruct(((STEP + 1) * modes, LANE_TILE, chans), F32),
            jax.ShapeDtypeStruct((STEP, LANE_TILE, chans), F32),
            jax.ShapeDtypeStruct((chunks * modes, chans), F32),
            jax.ShapeDtypeStruct((2, modes, chans), F32),
        ),
        cost_estimate=pl.CostEstimate(flops=2_000_000, bytes_accessed=1_500_000, transcendentals=70_000),
        compiler_params=PARAMS,
    )(decay, residue, skip)


def full_dot(block_ref, weights):
    hops, pair, rows, chans = block_ref.shape
    depth = pair * chans
    total = None
    for hop in range(hops):
        left = jnp.concatenate([block_ref[hop, i] for i in range(pair)], axis=1)
        part = jnp.dot(left, weights(pl.ds(hop * depth, depth)), preferred_element_type=F32)
        total = part if total is None else total + part
    return total


def project_kernel(
    block_ref, weight_ref, power_ref, small_ref,
    query_ref, product_ref, carry_ref, state_ref, ends,
):
    rows, chans = product_ref.shape
    modes = small_ref.shape[1]
    chunks = rows // STEP

    both = full_dot(
        block_ref,
        lambda spot: jnp.concatenate([weight_ref[1, spot, :], weight_ref[2, spot, :]], axis=1),
    )
    keys = both[:, :chans].astype(BF16).astype(F32)
    values = both[:, chans:].astype(BF16).astype(F32)
    product_ref[...] = keys * values
    query = full_dot(block_ref, lambda spot: weight_ref[0, spot, :])
    query_ref[...] = query.astype(BF16).astype(F32)

    signal = [product_ref[pl.ds(j, chunks, stride=STEP), :] for j in range(STEP)]
    parts = chunks // LANE_TILE
    for m in range(modes):
        sums = [None] * parts
        for j in range(STEP):
            power = power_ref[(STEP - 1 - j) * modes + m]
            for h in range(parts):
                term = power * signal[j][h * LANE_TILE : (h + 1) * LANE_TILE, :]
                sums[h] = term if sums[h] is None else sums[h] + term
        ends[pl.ds(m, chunks, stride=modes), :] = jnp.concatenate(sums, axis=0)
    gain = small_ref[0]
    decay = small_ref[1]
    state = jnp.zeros((modes, chans), F32)
    for i in range(chunks):
        carry_ref[pl.ds(i * modes, modes), :] = state
        state = decay * state + gain * ends[pl.ds(i * modes, modes), :]
    state_ref[...] = state


def project(block, weight, power, small):
    rows, chans = block.shape[2:]
    modes = small.shape[1]
    chunks = rows // STEP
    return pl.pallas_call(
        project_kernel,
        out_shape=(
            jax.ShapeDtypeStruct((rows, chans), F32),
            jax.ShapeDtypeStruct((rows, chans), F32),
            jax.ShapeDtypeStruct((chunks * modes, chans), F32),
            jax.ShapeDtypeStruct((modes, chans), F32),
        ),
        scratch_shapes=[VMEM((chunks * modes, chans), F32)],
        compiler_params=PARAMS,
        cost_estimate=pl.CostEstimate(flops=410_000_000, bytes_accessed=4_000_000, transcendentals=0),
    )(block, weight, power, small)


def block_total_kernel(span, decay_ref, own_ref, twin_ref, total_ref):
    decay = jnp.exp(decay_ref[...] * (-float(span)))
    first = lax.axis_index("seq") % 2 == 0
    own = own_ref[...]
    twin = twin_ref[...]
    total = decay * jnp.where(first, own, twin) + jnp.where(first, twin, own)
    for i in range(total_ref.shape[0]):
        total_ref[i] = total


def block_total(decay, own, twin, span, copies):
    return pl.pallas_call(
        functools.partial(block_total_kernel, span),
        out_shape=jax.ShapeDtypeStruct((copies,) + own.shape, F32),
        compiler_params=PARAMS,
        cost_estimate=pl.CostEstimate(flops=10_000, bytes_accessed=300_000, transcendentals=2_048),
    )(decay, own, twin)


def combine_kernel(
    span, decay_ref, twin_ref, totals_ref, query_ref, product_ref, carry_ref,
    power_ref, impulse_ref, chunk_ref, copies_ref, states, result,
):
    pairs = totals_ref.shape[0]
    modes, chans = decay_ref.shape
    rows = product_ref.shape[0]
    chunks = rows // STEP
    parts = chunks // LANE_TILE
    place = lax.axis_index("seq")
    rate = decay_ref[...]
    decay = jnp.exp(rate * (-float(2 * span)))
    start = jnp.zeros((modes, chans), F32)
    for i in range(pairs - 1):
        start = jnp.where(i < place // 2, decay * start + totals_ref[i], start)
    later = jnp.exp(rate * (-float(span))) * start + twin_ref[...]
    start = jnp.where(place % 2 == 0, start, later)
    for i in range(chunks):
        spot = pl.ds(i * modes, modes)
        states[spot, :] = carry_ref[spot, :] + chunk_ref[spot, :] * start
    state = [states[pl.ds(m, chunks, stride=modes), :] for m in range(modes)]
    for j in range(STEP):
        sums = [None] * parts
        for m in range(modes):
            power = power_ref[(j + 1) * modes + m]
            for h in range(parts):
                term = power * state[m][h * LANE_TILE : (h + 1) * LANE_TILE, :]
                sums[h] = term if sums[h] is None else sums[h] + term
        result[pl.ds(j, chunks, stride=STEP), :] = jnp.concatenate(sums, axis=0)
    signal = [product_ref[pl.ds(j, chunks, stride=STEP), :] for j in range(STEP)]
    for j in range(STEP):
        spot = pl.ds(j, chunks, stride=STEP)
        sums = [None] * parts
        for k in range(j + 1):
            tap = impulse_ref[k]
            for h in range(parts):
                term = tap * signal[j - k][h * LANE_TILE : (h + 1) * LANE_TILE, :]
                sums[h] = term if sums[h] is None else sums[h] + term
        result[spot, :] = (result[spot, :] + jnp.concatenate(sums, axis=0)) * query_ref[spot, :]
    mixed = result[...].astype(BF16)
    for i in range(copies_ref.shape[0]):
        copies_ref[i] = mixed


def combine(decay, twin, totals, query, product, carry, power, impulse, chunk, copies):
    rows, chans = product.shape
    return pl.pallas_call(
        functools.partial(combine_kernel, rows),
        out_shape=jax.ShapeDtypeStruct((copies, rows, chans), BF16),
        scratch_shapes=[VMEM(carry.shape, F32), VMEM((rows, chans), F32)],
        compiler_params=PARAMS,
        cost_estimate=pl.CostEstimate(flops=3_000_000, bytes_accessed=3_000_000, transcendentals=10_000),
    )(decay, twin, totals, query, product, carry, power, impulse, chunk)


def partial_kernel(near_ref, weight_ref, out_ref):
    hops, rows, chans = near_ref.shape
    total = None
    for hop in range(0, hops, 2):
        width = min(2, hops - hop)
        left = jnp.concatenate([near_ref[hop + i] for i in range(width)], axis=1)
        right = weight_ref[pl.ds(hop * chans, width * chans), :]
        part = jnp.dot(left, right, preferred_element_type=F32)
        total = part if total is None else total + part
    out_ref[...] = total.astype(out_ref.dtype)


def partial_output(near, weight, dtype):
    rows = near.shape[1]
    return pl.pallas_call(
        partial_kernel,
        out_shape=jax.ShapeDtypeStruct((rows, weight.shape[1]), dtype),
        compiler_params=PARAMS,
        cost_estimate=pl.CostEstimate(flops=70_000_000, bytes_accessed=900_000, transcendentals=0),
    )(near, weight)


def copied(block, count):
    return jnp.broadcast_to(block[None], (count,) + block.shape)


def exchange(copies, axis, groups):
    return lax.all_to_all(copies, axis, 0, 0, tiled=True, axis_index_groups=groups)


def on_device(tokens, in_weight, out_weight, decay_rates, residues, skip_gain):
    seq_count = lax.axis_size("seq")
    chan_count = lax.axis_size("chan")
    rows, chans = tokens.shape
    hops = chan_count // 2
    pairs = seq_count // 2
    same_core = [list(range(core, seq_count, 2)) for core in range(2)]
    same_half = [list(range(z, chan_count, 2)) for z in range(2)]
    both_halves = [[2 * x, 2 * x + 1] for x in range(hops)]
    other_core = [(i, i ^ 1) for i in range(seq_count)]
    other_half = [(c, c ^ 1) for c in range(chan_count)]

    half = lax.axis_index("chan") % 2
    stripes = out_weight.reshape(hops, 2, chans, out_weight.shape[1])
    own_weight = lax.dynamic_index_in_dim(stripes, half, 1, keepdims=False).reshape(hops * chans, -1)
    given = lax.dynamic_index_in_dim(stripes, 1 - half, 1, keepdims=False).reshape(hops * chans, -1)

    power, impulse, chunk, small = tables(decay_rates, residues, skip_gain[None, :], rows)
    paired = exchange(copied(tokens, 2), "chan", both_halves)
    paired, given = lax.optimization_barrier((paired, given))
    other_weight = lax.ppermute(given, "chan", other_half)
    block = exchange(copied(paired, hops), "chan", same_half)
    block, other_weight = lax.optimization_barrier((block, other_weight))
    query, product, carry, state = project(block, in_weight, power, small)
    twin = lax.ppermute(state, "seq", other_core)
    totals = exchange(block_total(decay_rates, state, twin, rows, pairs), "seq", same_core)
    copies = combine(
        decay_rates, twin, totals, query, product, carry, power, impulse, chunk, hops
    )
    near = exchange(copies, "chan", same_half)
    theirs = lax.ppermute(partial_output(near, other_weight, BF16), "chan", other_half)
    ours = partial_output(near, own_weight, F32)
    return (ours + theirs.astype(F32)).astype(BF16)


def solution(mesh):
    return jax.shard_map(
        on_device,
        mesh=mesh,
        in_specs=(
            P("seq", "chan"),
            P(None, None, "chan"),
            P(None, "chan"),
            P(None, "chan"),
            P(None, "chan"),
            P("chan"),
        ),
        out_specs=P("seq", "chan"),
        check_vma=False,
    )
```

```python
import functools

import jax
import jax.numpy as jnp
from jax import lax
from jax.experimental import pallas as pl
from jax.experimental.pallas import tpu as pltpu
from jax.sharding import PartitionSpec as P


F32 = jnp.float32
BF16 = jnp.bfloat16
VMEM = pltpu.VMEM
STEP = 16
LANE_TILE = 8
PARAMS = pltpu.CompilerParams(vmem_limit_bytes=12 * 1024 * 1024)


def table_kernel(
    decay_ref, residue_ref, skip_ref, ahead_ref, power_ref, impulse_ref, chunk_ref, small_ref
):
    rate = decay_ref[...]
    modes, chans = rate.shape
    chunks = chunk_ref.shape[0] // modes
    gain = residue_ref[...] * jnp.sqrt(2.0 * rate)
    for k in range(STEP + 1):
        power = jnp.exp(rate * (-float(k)))
        for m in range(modes):
            power_ref[k * modes + m] = jnp.broadcast_to(power[m : m + 1, :], (LANE_TILE, chans))
        if k < STEP:
            tap = jnp.sum(gain * power, axis=0, keepdims=True)
            if k == 0:
                tap = tap + skip_ref[...]
            impulse_ref[k] = jnp.broadcast_to(tap, (LANE_TILE, chans))
    for i in range(chunks):
        chunk_ref[pl.ds(i * modes, modes), :] = jnp.exp(rate * (-float(STEP * i)))
    small_ref[0] = gain
    small_ref[1] = jnp.exp(rate * (-float(STEP)))


def tables(decay, residue, skip, ahead, rows):
    modes, chans = decay.shape
    chunks = rows // STEP
    return pl.pallas_call(
        table_kernel,
        in_specs=[pl.BlockSpec(memory_space=VMEM)] * 3 + [pl.BlockSpec(memory_space=pl.ANY)],
        out_shape=(
            jax.ShapeDtypeStruct(((STEP + 1) * modes, LANE_TILE, chans), F32),
            jax.ShapeDtypeStruct((STEP, LANE_TILE, chans), F32),
            jax.ShapeDtypeStruct((chunks * modes, chans), F32),
            jax.ShapeDtypeStruct((2, modes, chans), F32),
        ),
        cost_estimate=pl.CostEstimate(flops=2_000_000, bytes_accessed=1_500_000, transcendentals=70_000),
        compiler_params=PARAMS,
    )(decay, residue, skip, ahead)


def spread_kernel(own_ref, swapped_ref, copies_ref):
    own = own_ref[...]
    swapped = swapped_ref[...]
    for i in range(copies_ref.shape[0]):
        copies_ref[i, 0] = own
        copies_ref[i, 1] = swapped


def spread(own, swapped, count):
    return pl.pallas_call(
        spread_kernel,
        out_shape=jax.ShapeDtypeStruct((count, 2) + own.shape, own.dtype),
        compiler_params=PARAMS,
        cost_estimate=pl.CostEstimate(flops=0, bytes_accessed=1_200_000, transcendentals=0),
    )(own, swapped)


def project_kernel(
    block_ref, weight_ref, power_ref, small_ref,
    query_ref, product_ref, carry_ref, state_ref, ends,
):
    rows, chans = product_ref.shape
    hops, pair = block_ref.shape[:2]
    modes = small_ref.shape[1]
    chunks = rows // STEP

    half = lax.axis_index("chan") % 2
    both = None
    query = None
    for hop in range(hops):
        near = pl.ds(pl.multiple_of((pair * hop + half) * chans, chans), chans)
        far = pl.ds(pl.multiple_of((pair * hop + 1 - half) * chans, chans), chans)
        left = jnp.concatenate([block_ref[hop, i] for i in range(pair)], axis=1)
        rights = [
            jnp.concatenate([weight_ref[i, near, :], weight_ref[i, far, :]], axis=0) for i in range(3)
        ]
        pair_part = jnp.dot(
            left, jnp.concatenate(rights[1:], axis=1), preferred_element_type=F32
        )
        query_part = jnp.dot(left, rights[0], preferred_element_type=F32)
        both = pair_part if both is None else both + pair_part
        query = query_part if query is None else query + query_part
    keys = both[:, :chans].astype(BF16).astype(F32)
    values = both[:, chans:].astype(BF16).astype(F32)
    product_ref[...] = keys * values
    query_ref[...] = query.astype(BF16).astype(F32)

    signal = [product_ref[pl.ds(j, chunks, stride=STEP), :] for j in range(STEP)]
    parts = chunks // LANE_TILE
    for m in range(modes):
        sums = [None] * parts
        for j in range(STEP):
            power = power_ref[(STEP - 1 - j) * modes + m]
            for h in range(parts):
                term = power * signal[j][h * LANE_TILE : (h + 1) * LANE_TILE, :]
                sums[h] = term if sums[h] is None else sums[h] + term
        ends[pl.ds(m, chunks, stride=modes), :] = jnp.concatenate(sums, axis=0)
    gain = small_ref[0]
    decay = small_ref[1]
    state = jnp.zeros((modes, chans), F32)
    for i in range(chunks):
        carry_ref[pl.ds(i * modes, modes), :] = state
        state = decay * state + gain * ends[pl.ds(i * modes, modes), :]
    state_ref[...] = state


def project(block, weight, power, small):
    rows, chans = block.shape[2:]
    modes = small.shape[1]
    chunks = rows // STEP
    return pl.pallas_call(
        project_kernel,
        out_shape=(
            jax.ShapeDtypeStruct((rows, chans), F32),
            jax.ShapeDtypeStruct((rows, chans), F32),
            jax.ShapeDtypeStruct((chunks * modes, chans), F32),
            jax.ShapeDtypeStruct((modes, chans), F32),
        ),
        scratch_shapes=[VMEM((chunks * modes, chans), F32)],
        compiler_params=PARAMS,
        cost_estimate=pl.CostEstimate(flops=410_000_000, bytes_accessed=4_000_000, transcendentals=0),
    )(block, weight, power, small)


def block_total_kernel(span, decay_ref, own_ref, twin_ref, total_ref):
    decay = jnp.exp(decay_ref[...] * (-float(span)))
    first = lax.axis_index("seq") % 2 == 0
    own = own_ref[...]
    twin = twin_ref[...]
    total = decay * jnp.where(first, own, twin) + jnp.where(first, twin, own)
    for i in range(total_ref.shape[0]):
        total_ref[i] = total


def block_total(decay, own, twin, span, copies):
    return pl.pallas_call(
        functools.partial(block_total_kernel, span),
        out_shape=jax.ShapeDtypeStruct((copies,) + own.shape, F32),
        compiler_params=PARAMS,
        cost_estimate=pl.CostEstimate(flops=10_000, bytes_accessed=300_000, transcendentals=2_048),
    )(decay, own, twin)


def combine_kernel(
    span, decay_ref, twin_ref, totals_ref, query_ref, product_ref, carry_ref,
    power_ref, impulse_ref, chunk_ref, copies_ref, states, result,
):
    pairs = totals_ref.shape[0]
    modes, chans = decay_ref.shape
    rows = product_ref.shape[0]
    chunks = rows // STEP
    parts = chunks // LANE_TILE
    place = lax.axis_index("seq")
    rate = decay_ref[...]
    decay = jnp.exp(rate * (-float(2 * span)))
    start = jnp.zeros((modes, chans), F32)
    for i in range(pairs - 1):
        start = jnp.where(i < place // 2, decay * start + totals_ref[i], start)
    later = jnp.exp(rate * (-float(span))) * start + twin_ref[...]
    start = jnp.where(place % 2 == 0, start, later)
    for i in range(chunks):
        spot = pl.ds(i * modes, modes)
        states[spot, :] = carry_ref[spot, :] + chunk_ref[spot, :] * start
    state = [states[pl.ds(m, chunks, stride=modes), :] for m in range(modes)]
    for j in range(STEP):
        sums = [None] * parts
        for m in range(modes):
            power = power_ref[(j + 1) * modes + m]
            for h in range(parts):
                term = power * state[m][h * LANE_TILE : (h + 1) * LANE_TILE, :]
                sums[h] = term if sums[h] is None else sums[h] + term
        result[pl.ds(j, chunks, stride=STEP), :] = jnp.concatenate(sums, axis=0)
    signal = [product_ref[pl.ds(j, chunks, stride=STEP), :] for j in range(STEP)]
    for j in range(STEP):
        spot = pl.ds(j, chunks, stride=STEP)
        sums = [None] * parts
        for k in range(j + 1):
            tap = impulse_ref[k]
            for h in range(parts):
                term = tap * signal[j - k][h * LANE_TILE : (h + 1) * LANE_TILE, :]
                sums[h] = term if sums[h] is None else sums[h] + term
        result[spot, :] = (result[spot, :] + jnp.concatenate(sums, axis=0)) * query_ref[spot, :]
    mixed = result[...].astype(BF16)
    for i in range(copies_ref.shape[0]):
        copies_ref[i] = mixed


def combine(decay, twin, totals, query, product, carry, power, impulse, chunk, copies):
    rows, chans = product.shape
    return pl.pallas_call(
        functools.partial(combine_kernel, rows),
        out_shape=jax.ShapeDtypeStruct((copies, rows, chans), BF16),
        scratch_shapes=[VMEM(carry.shape, F32), VMEM((rows, chans), F32)],
        compiler_params=PARAMS,
        cost_estimate=pl.CostEstimate(flops=3_000_000, bytes_accessed=3_000_000, transcendentals=10_000),
    )(decay, twin, totals, query, product, carry, power, impulse, chunk)


def partial_kernel(near_ref, weight_ref, out_ref):
    hops, rows, chans = near_ref.shape
    total = None
    for hop in range(0, hops, 2):
        width = min(2, hops - hop)
        left = jnp.concatenate([near_ref[hop + i] for i in range(width)], axis=1)
        right = weight_ref[pl.ds(hop * chans, width * chans), :]
        part = jnp.dot(left, right, preferred_element_type=F32)
        total = part if total is None else total + part
    out_ref[...] = total.astype(out_ref.dtype)


def partial_output(near, weight, dtype):
    rows = near.shape[1]
    return pl.pallas_call(
        partial_kernel,
        out_shape=jax.ShapeDtypeStruct((rows, weight.shape[1]), dtype),
        compiler_params=PARAMS,
        cost_estimate=pl.CostEstimate(flops=70_000_000, bytes_accessed=900_000, transcendentals=0),
    )(near, weight)


def exchange(copies, axis, groups):
    return lax.all_to_all(copies, axis, 0, 0, tiled=True, axis_index_groups=groups)


def on_device(tokens, in_weight, out_weight, decay_rates, residues, skip_gain):
    seq_count = lax.axis_size("seq")
    chan_count = lax.axis_size("chan")
    rows, chans = tokens.shape
    hops = chan_count // 2
    pairs = seq_count // 2
    same_core = [list(range(core, seq_count, 2)) for core in range(2)]
    same_half = [list(range(z, chan_count, 2)) for z in range(2)]
    other_core = [(i, i ^ 1) for i in range(seq_count)]
    other_half = [(c, c ^ 1) for c in range(chan_count)]

    swapped = lax.ppermute(tokens, "chan", other_half)
    copies = spread(tokens, swapped, hops)
    copies, late_weight = lax.optimization_barrier((copies, out_weight))
    half = lax.axis_index("chan") % 2
    stripes = late_weight.reshape(hops, 2, chans, out_weight.shape[1])
    own_weight = lax.dynamic_index_in_dim(stripes, half, 1, keepdims=False).reshape(hops * chans, -1)
    given = lax.dynamic_index_in_dim(stripes, 1 - half, 1, keepdims=False).reshape(hops * chans, -1)
    other_weight = lax.ppermute(given, "chan", other_half)
    power, impulse, chunk, small = tables(
        decay_rates, residues, skip_gain[None, :], in_weight, rows
    )
    block = exchange(copies, "chan", same_half)
    block, other_weight = lax.optimization_barrier((block, other_weight))
    query, product, carry, state = project(block, in_weight, power, small)
    twin = lax.ppermute(state, "seq", other_core)
    totals = exchange(block_total(decay_rates, state, twin, rows, pairs), "seq", same_core)
    copies = combine(
        decay_rates, twin, totals, query, product, carry, power, impulse, chunk, hops
    )
    near = exchange(copies, "chan", same_half)
    theirs = lax.ppermute(partial_output(near, other_weight, BF16), "chan", other_half)
    ours = partial_output(near, own_weight, F32)
    return (ours + theirs.astype(F32)).astype(BF16)


def solution(mesh):
    return jax.shard_map(
        on_device,
        mesh=mesh,
        in_specs=(
            P("seq", "chan"),
            P(None, None, "chan"),
            P(None, "chan"),
            P(None, "chan"),
            P(None, "chan"),
            P("chan"),
        ),
        out_specs=P("seq", "chan"),
        check_vma=False,
    )
```

```python
import functools

import jax
import jax.numpy as jnp
from jax import lax
from jax.experimental import pallas as pl
from jax.experimental.pallas import tpu as pltpu
from jax.sharding import PartitionSpec as P


F32 = jnp.float32
BF16 = jnp.bfloat16
VMEM = pltpu.VMEM
STEP = 16
LANE_TILE = 8
PARAMS = pltpu.CompilerParams(vmem_limit_bytes=12 * 1024 * 1024)


def table_kernel(
    decay_ref, residue_ref, skip_ref, ahead_ref, power_ref, impulse_ref, chunk_ref, small_ref
):
    rate = decay_ref[...]
    modes, chans = rate.shape
    chunks = chunk_ref.shape[0] // modes
    gain = residue_ref[...] * jnp.sqrt(2.0 * rate)
    for k in range(STEP + 1):
        power = jnp.exp(rate * (-float(k)))
        for m in range(modes):
            power_ref[k * modes + m] = jnp.broadcast_to(power[m : m + 1, :], (LANE_TILE, chans))
        if k < STEP:
            tap = jnp.sum(gain * power, axis=0, keepdims=True)
            if k == 0:
                tap = tap + skip_ref[...]
            impulse_ref[k] = jnp.broadcast_to(tap, (LANE_TILE, chans))
    for i in range(chunks):
        chunk_ref[pl.ds(i * modes, modes), :] = jnp.exp(rate * (-float(STEP * i)))
    small_ref[0] = gain
    small_ref[1] = jnp.exp(rate * (-float(STEP)))


def tables(decay, residue, skip, ahead, rows):
    modes, chans = decay.shape
    chunks = rows // STEP
    return pl.pallas_call(
        table_kernel,
        in_specs=[pl.BlockSpec(memory_space=VMEM)] * 3 + [pl.BlockSpec(memory_space=pl.ANY)],
        out_shape=(
            jax.ShapeDtypeStruct(((STEP + 1) * modes, LANE_TILE, chans), F32),
            jax.ShapeDtypeStruct((STEP, LANE_TILE, chans), F32),
            jax.ShapeDtypeStruct((chunks * modes, chans), F32),
            jax.ShapeDtypeStruct((2, modes, chans), F32),
        ),
        cost_estimate=pl.CostEstimate(flops=2_000_000, bytes_accessed=1_500_000, transcendentals=70_000),
        compiler_params=PARAMS,
    )(decay, residue, skip, ahead)


def hold_kernel(block_ref, held_ref):
    held_ref[...] = block_ref[...]


def hold(block):
    return pl.pallas_call(
        hold_kernel,
        out_shape=jax.ShapeDtypeStruct(block.shape, block.dtype),
        compiler_params=PARAMS,
        cost_estimate=pl.CostEstimate(flops=0, bytes_accessed=130_000, transcendentals=0),
    )(block)


def spread_kernel(own_ref, swapped_ref, copies_ref):
    own = own_ref[...]
    swapped = swapped_ref[...]
    for i in range(copies_ref.shape[0]):
        copies_ref[i, 0] = own
        copies_ref[i, 1] = swapped


def spread(own, swapped, count):
    return pl.pallas_call(
        spread_kernel,
        out_shape=jax.ShapeDtypeStruct((count, 2) + own.shape, own.dtype),
        compiler_params=PARAMS,
        cost_estimate=pl.CostEstimate(flops=0, bytes_accessed=1_200_000, transcendentals=0),
    )(own, swapped)


def project_kernel(
    block_ref, weight_ref, power_ref, small_ref,
    query_ref, product_ref, carry_ref, state_ref, ends,
):
    rows, chans = product_ref.shape
    hops, pair = block_ref.shape[:2]
    modes = small_ref.shape[1]
    chunks = rows // STEP

    half = lax.axis_index("chan") % 2
    both = None
    query = None
    for hop in range(hops):
        near = pl.ds(pl.multiple_of((pair * hop + half) * chans, chans), chans)
        far = pl.ds(pl.multiple_of((pair * hop + 1 - half) * chans, chans), chans)
        left = jnp.concatenate([block_ref[hop, i] for i in range(pair)], axis=1)
        rights = [
            jnp.concatenate([weight_ref[i, near, :], weight_ref[i, far, :]], axis=0) for i in range(3)
        ]
        pair_part = jnp.dot(
            left, jnp.concatenate(rights[1:], axis=1), preferred_element_type=F32
        )
        query_part = jnp.dot(left, rights[0], preferred_element_type=F32)
        both = pair_part if both is None else both + pair_part
        query = query_part if query is None else query + query_part
    keys = both[:, :chans].astype(BF16).astype(F32)
    values = both[:, chans:].astype(BF16).astype(F32)
    product_ref[...] = keys * values
    query_ref[...] = query.astype(BF16).astype(F32)

    signal = [product_ref[pl.ds(j, chunks, stride=STEP), :] for j in range(STEP)]
    parts = chunks // LANE_TILE
    for m in range(modes):
        sums = [None] * parts
        for j in range(STEP):
            power = power_ref[(STEP - 1 - j) * modes + m]
            for h in range(parts):
                term = power * signal[j][h * LANE_TILE : (h + 1) * LANE_TILE, :]
                sums[h] = term if sums[h] is None else sums[h] + term
        ends[pl.ds(m, chunks, stride=modes), :] = jnp.concatenate(sums, axis=0)
    gain = small_ref[0]
    decay = small_ref[1]
    state = jnp.zeros((modes, chans), F32)
    for i in range(chunks):
        carry_ref[pl.ds(i * modes, modes), :] = state
        state = decay * state + gain * ends[pl.ds(i * modes, modes), :]
    rounded = state.astype(state_ref.dtype)
    for i in range(state_ref.shape[0]):
        state_ref[i] = rounded


def project(block, weight, power, small, copies):
    rows, chans = block.shape[2:]
    modes = small.shape[1]
    chunks = rows // STEP
    return pl.pallas_call(
        project_kernel,
        out_shape=(
            jax.ShapeDtypeStruct((rows, chans), F32),
            jax.ShapeDtypeStruct((rows, chans), F32),
            jax.ShapeDtypeStruct((chunks * modes, chans), F32),
            jax.ShapeDtypeStruct((copies, modes, chans), BF16),
        ),
        scratch_shapes=[VMEM((chunks * modes, chans), F32)],
        compiler_params=PARAMS,
        cost_estimate=pl.CostEstimate(flops=410_000_000, bytes_accessed=4_000_000, transcendentals=0),
    )(block, weight, power, small)


def combine_kernel(
    span, decay_ref, states_ref, query_ref, product_ref, carry_ref,
    power_ref, impulse_ref, chunk_ref, copies_ref, entry, result,
):
    blocks = states_ref.shape[0]
    modes, chans = decay_ref.shape
    rows = product_ref.shape[0]
    chunks = rows // STEP
    parts = chunks // LANE_TILE
    place = lax.axis_index("seq")
    rate = decay_ref[...]
    decay = jnp.exp(rate * (-float(span)))
    start = jnp.zeros((modes, chans), F32)
    for i in range(blocks - 1):
        start = jnp.where(i < place, decay * start + states_ref[i].astype(F32), start)
    for i in range(chunks):
        spot = pl.ds(i * modes, modes)
        entry[spot, :] = carry_ref[spot, :] + chunk_ref[spot, :] * start
    state = [entry[pl.ds(m, chunks, stride=modes), :] for m in range(modes)]
    for j in range(STEP):
        sums = [None] * parts
        for m in range(modes):
            power = power_ref[(j + 1) * modes + m]
            for h in range(parts):
                term = power * state[m][h * LANE_TILE : (h + 1) * LANE_TILE, :]
                sums[h] = term if sums[h] is None else sums[h] + term
        result[pl.ds(j, chunks, stride=STEP), :] = jnp.concatenate(sums, axis=0)
    signal = [product_ref[pl.ds(j, chunks, stride=STEP), :] for j in range(STEP)]
    for j in range(STEP):
        spot = pl.ds(j, chunks, stride=STEP)
        sums = [None] * parts
        for k in range(j + 1):
            tap = impulse_ref[k]
            for h in range(parts):
                term = tap * signal[j - k][h * LANE_TILE : (h + 1) * LANE_TILE, :]
                sums[h] = term if sums[h] is None else sums[h] + term
        result[spot, :] = (result[spot, :] + jnp.concatenate(sums, axis=0)) * query_ref[spot, :]
    mixed = result[...].astype(BF16)
    for i in range(copies_ref.shape[0]):
        copies_ref[i] = mixed


def combine(decay, states, query, product, carry, power, impulse, chunk, copies):
    rows, chans = product.shape
    return pl.pallas_call(
        functools.partial(combine_kernel, rows),
        out_shape=jax.ShapeDtypeStruct((copies, rows, chans), BF16),
        scratch_shapes=[VMEM(carry.shape, F32), VMEM((rows, chans), F32)],
        compiler_params=PARAMS,
        cost_estimate=pl.CostEstimate(flops=3_000_000, bytes_accessed=3_000_000, transcendentals=10_000),
    )(decay, states, query, product, carry, power, impulse, chunk)


def partial_kernel(near_ref, weight_ref, out_ref):
    hops, rows, chans = near_ref.shape
    total = None
    for hop in range(0, hops, 2):
        width = min(2, hops - hop)
        left = jnp.concatenate([near_ref[hop + i] for i in range(width)], axis=1)
        right = weight_ref[pl.ds(hop * chans, width * chans), :]
        part = jnp.dot(left, right, preferred_element_type=F32)
        total = part if total is None else total + part
    out_ref[...] = total.astype(out_ref.dtype)


def partial_output(near, weight, dtype):
    rows = near.shape[1]
    return pl.pallas_call(
        partial_kernel,
        out_shape=jax.ShapeDtypeStruct((rows, weight.shape[1]), dtype),
        compiler_params=PARAMS,
        cost_estimate=pl.CostEstimate(flops=70_000_000, bytes_accessed=900_000, transcendentals=0),
    )(near, weight)


def exchange(copies, axis, groups):
    return lax.all_to_all(copies, axis, 0, 0, tiled=True, axis_index_groups=groups)


def on_device(tokens, in_weight, out_weight, decay_rates, residues, skip_gain):
    seq_count = lax.axis_size("seq")
    chan_count = lax.axis_size("chan")
    rows, chans = tokens.shape
    hops = chan_count // 2
    same_half = [list(range(z, chan_count, 2)) for z in range(2)]
    other_half = [(c, c ^ 1) for c in range(chan_count)]

    swapped = lax.ppermute(tokens, "chan", other_half)
    copies = spread(hold(tokens), swapped, hops)
    copies, late_weight = lax.optimization_barrier((copies, out_weight))
    half = lax.axis_index("chan") % 2
    stripes = late_weight.reshape(hops, 2, chans, out_weight.shape[1])
    own_weight = lax.dynamic_index_in_dim(stripes, half, 1, keepdims=False).reshape(hops * chans, -1)
    given = lax.dynamic_index_in_dim(stripes, 1 - half, 1, keepdims=False).reshape(hops * chans, -1)
    other_weight = lax.ppermute(given, "chan", other_half)
    power, impulse, chunk, small = tables(
        decay_rates, residues, skip_gain[None, :], in_weight, rows
    )
    block = exchange(copies, "chan", same_half)
    block, other_weight = lax.optimization_barrier((block, other_weight))
    query, product, carry, states = project(block, in_weight, power, small, seq_count)
    states = lax.all_to_all(states, "seq", 0, 0, tiled=True)
    copies = combine(decay_rates, states, query, product, carry, power, impulse, chunk, hops)
    near = exchange(copies, "chan", same_half)
    theirs = lax.ppermute(partial_output(near, other_weight, BF16), "chan", other_half)
    ours = partial_output(near, own_weight, F32)
    return (ours + theirs.astype(F32)).astype(BF16)


def solution(mesh):
    return jax.shard_map(
        on_device,
        mesh=mesh,
        in_specs=(
            P("seq", "chan"),
            P(None, None, "chan"),
            P(None, "chan"),
            P(None, "chan"),
            P(None, "chan"),
            P("chan"),
        ),
        out_specs=P("seq", "chan"),
        check_vma=False,
    )
```

```python
import functools

import jax
import jax.numpy as jnp
from jax import lax
from jax.experimental import pallas as pl
from jax.experimental.pallas import tpu as pltpu
from jax.sharding import PartitionSpec as P


F32 = jnp.float32
BF16 = jnp.bfloat16
VMEM = pltpu.VMEM
STEP = 16
LANE_TILE = 8
PARAMS = pltpu.CompilerParams(vmem_limit_bytes=12 * 1024 * 1024)


def table_kernel(
    decay_ref, residue_ref, skip_ref, ahead_ref, power_ref, impulse_ref, chunk_ref, small_ref
):
    rate = decay_ref[...]
    modes, chans = rate.shape
    chunks = chunk_ref.shape[0] // modes
    gain = residue_ref[...] * jnp.sqrt(2.0 * rate)
    for k in range(STEP + 1):
        power = jnp.exp(rate * (-float(k)))
        for m in range(modes):
            power_ref[k * modes + m] = jnp.broadcast_to(power[m : m + 1, :], (LANE_TILE, chans))
        if k < STEP:
            tap = jnp.sum(gain * power, axis=0, keepdims=True)
            if k == 0:
                tap = tap + skip_ref[...]
            impulse_ref[k] = jnp.broadcast_to(tap, (LANE_TILE, chans))
    for i in range(chunks):
        chunk_ref[pl.ds(i * modes, modes), :] = jnp.exp(rate * (-float(STEP * i)))
    small_ref[0] = gain
    small_ref[1] = jnp.exp(rate * (-float(STEP)))


def tables(decay, residue, skip, ahead, rows):
    modes, chans = decay.shape
    chunks = rows // STEP
    return pl.pallas_call(
        table_kernel,
        in_specs=[pl.BlockSpec(memory_space=VMEM)] * 3 + [pl.BlockSpec(memory_space=pl.ANY)],
        out_shape=(
            jax.ShapeDtypeStruct(((STEP + 1) * modes, LANE_TILE, chans), F32),
            jax.ShapeDtypeStruct((STEP, LANE_TILE, chans), F32),
            jax.ShapeDtypeStruct((chunks * modes, chans), F32),
            jax.ShapeDtypeStruct((2, modes, chans), F32),
        ),
        cost_estimate=pl.CostEstimate(flops=2_000_000, bytes_accessed=1_500_000, transcendentals=70_000),
        compiler_params=PARAMS,
    )(decay, residue, skip, ahead)


def hold_kernel(block_ref, held_ref):
    held_ref[...] = block_ref[...]


def hold(block):
    return pl.pallas_call(
        hold_kernel,
        out_shape=jax.ShapeDtypeStruct(block.shape, block.dtype),
        compiler_params=PARAMS,
        cost_estimate=pl.CostEstimate(flops=0, bytes_accessed=130_000, transcendentals=0),
    )(block)


def spread_kernel(own_ref, swapped_ref, copies_ref):
    own = own_ref[...]
    swapped = swapped_ref[...]
    for i in range(copies_ref.shape[0]):
        copies_ref[i, 0] = own
        copies_ref[i, 1] = swapped


def spread(own, swapped, count):
    return pl.pallas_call(
        spread_kernel,
        out_shape=jax.ShapeDtypeStruct((count, 2) + own.shape, own.dtype),
        compiler_params=PARAMS,
        cost_estimate=pl.CostEstimate(flops=0, bytes_accessed=1_200_000, transcendentals=0),
    )(own, swapped)


def project_kernel(
    block_ref, weight_ref, power_ref, small_ref,
    query_ref, product_ref, carry_ref, state_ref, ends, held, arrived,
):
    rows, chans = product_ref.shape
    hops, pair = block_ref.shape[:2]
    modes = small_ref.shape[1]
    chunks = rows // STEP

    copies = [
        pltpu.make_async_copy(block_ref.at[hop], held.at[hop], arrived.at[hop])
        for hop in range(hops)
    ]
    for copy in copies:
        copy.start()
    half = lax.axis_index("chan") % 2
    both = None
    query = None
    for hop in range(hops):
        near = pl.ds(pl.multiple_of((pair * hop + half) * chans, chans), chans)
        far = pl.ds(pl.multiple_of((pair * hop + 1 - half) * chans, chans), chans)
        copies[hop].wait()
        left = jnp.concatenate([held[hop, i] for i in range(pair)], axis=1)
        rights = [
            jnp.concatenate([weight_ref[i, near, :], weight_ref[i, far, :]], axis=0) for i in range(3)
        ]
        pair_part = jnp.dot(
            left, jnp.concatenate(rights[1:], axis=1), preferred_element_type=F32
        )
        query_part = jnp.dot(left, rights[0], preferred_element_type=F32)
        both = pair_part if both is None else both + pair_part
        query = query_part if query is None else query + query_part
    keys = both[:, :chans].astype(BF16).astype(F32)
    values = both[:, chans:].astype(BF16).astype(F32)
    product_ref[...] = keys * values
    query_ref[...] = query.astype(BF16).astype(F32)

    signal = [product_ref[pl.ds(j, chunks, stride=STEP), :] for j in range(STEP)]
    parts = chunks // LANE_TILE
    for m in range(modes):
        sums = [None] * parts
        for j in range(STEP):
            power = power_ref[(STEP - 1 - j) * modes + m]
            for h in range(parts):
                term = power * signal[j][h * LANE_TILE : (h + 1) * LANE_TILE, :]
                sums[h] = term if sums[h] is None else sums[h] + term
        ends[pl.ds(m, chunks, stride=modes), :] = jnp.concatenate(sums, axis=0)
    gain = small_ref[0]
    decay = small_ref[1]
    state = jnp.zeros((modes, chans), F32)
    for i in range(chunks):
        carry_ref[pl.ds(i * modes, modes), :] = state
        state = decay * state + gain * ends[pl.ds(i * modes, modes), :]
    rounded = state.astype(state_ref.dtype)
    for i in range(state_ref.shape[0]):
        state_ref[i] = rounded


def project(block, weight, power, small, copies):
    rows, chans = block.shape[2:]
    modes = small.shape[1]
    chunks = rows // STEP
    return pl.pallas_call(
        project_kernel,
        in_specs=[pl.BlockSpec(memory_space=pl.ANY)] + [pl.BlockSpec(memory_space=VMEM)] * 3,
        out_shape=(
            jax.ShapeDtypeStruct((rows, chans), F32),
            jax.ShapeDtypeStruct((rows, chans), F32),
            jax.ShapeDtypeStruct((chunks * modes, chans), F32),
            jax.ShapeDtypeStruct((copies, modes, chans), BF16),
        ),
        scratch_shapes=[
            VMEM((chunks * modes, chans), F32),
            VMEM(block.shape, BF16),
            pltpu.SemaphoreType.DMA((block.shape[0],)),
        ],
        compiler_params=PARAMS,
        cost_estimate=pl.CostEstimate(flops=410_000_000, bytes_accessed=4_000_000, transcendentals=0),
    )(block, weight, power, small)


def combine_kernel(
    span, decay_ref, states_ref, query_ref, product_ref, carry_ref,
    power_ref, impulse_ref, chunk_ref, copies_ref, entry, result,
):
    blocks = states_ref.shape[0]
    modes, chans = decay_ref.shape
    rows = product_ref.shape[0]
    chunks = rows // STEP
    parts = chunks // LANE_TILE
    place = lax.axis_index("seq")
    rate = decay_ref[...]
    decay = jnp.exp(rate * (-float(span)))
    start = jnp.zeros((modes, chans), F32)
    for i in range(blocks - 1):
        start = jnp.where(i < place, decay * start + states_ref[i].astype(F32), start)
    for i in range(chunks):
        spot = pl.ds(i * modes, modes)
        entry[spot, :] = carry_ref[spot, :] + chunk_ref[spot, :] * start
    state = [entry[pl.ds(m, chunks, stride=modes), :] for m in range(modes)]
    for j in range(STEP):
        sums = [None] * parts
        for m in range(modes):
            power = power_ref[(j + 1) * modes + m]
            for h in range(parts):
                term = power * state[m][h * LANE_TILE : (h + 1) * LANE_TILE, :]
                sums[h] = term if sums[h] is None else sums[h] + term
        result[pl.ds(j, chunks, stride=STEP), :] = jnp.concatenate(sums, axis=0)
    signal = [product_ref[pl.ds(j, chunks, stride=STEP), :] for j in range(STEP)]
    for j in range(STEP):
        spot = pl.ds(j, chunks, stride=STEP)
        sums = [None] * parts
        for k in range(j + 1):
            tap = impulse_ref[k]
            for h in range(parts):
                term = tap * signal[j - k][h * LANE_TILE : (h + 1) * LANE_TILE, :]
                sums[h] = term if sums[h] is None else sums[h] + term
        result[spot, :] = (result[spot, :] + jnp.concatenate(sums, axis=0)) * query_ref[spot, :]
    mixed = result[...].astype(BF16)
    for i in range(copies_ref.shape[0]):
        copies_ref[i] = mixed


def combine(decay, states, query, product, carry, power, impulse, chunk, copies):
    rows, chans = product.shape
    return pl.pallas_call(
        functools.partial(combine_kernel, rows),
        out_shape=jax.ShapeDtypeStruct((copies, rows, chans), BF16),
        scratch_shapes=[VMEM(carry.shape, F32), VMEM((rows, chans), F32)],
        compiler_params=PARAMS,
        cost_estimate=pl.CostEstimate(flops=3_000_000, bytes_accessed=3_000_000, transcendentals=10_000),
    )(decay, states, query, product, carry, power, impulse, chunk)


def partial_kernel(near_ref, weight_ref, out_ref):
    hops, rows, chans = near_ref.shape
    total = None
    for hop in range(0, hops, 2):
        width = min(2, hops - hop)
        left = jnp.concatenate([near_ref[hop + i] for i in range(width)], axis=1)
        right = weight_ref[pl.ds(hop * chans, width * chans), :]
        part = jnp.dot(left, right, preferred_element_type=F32)
        total = part if total is None else total + part
    out_ref[...] = total.astype(out_ref.dtype)


def partial_output(near, weight, dtype):
    rows = near.shape[1]
    return pl.pallas_call(
        partial_kernel,
        out_shape=jax.ShapeDtypeStruct((rows, weight.shape[1]), dtype),
        compiler_params=PARAMS,
        cost_estimate=pl.CostEstimate(flops=70_000_000, bytes_accessed=900_000, transcendentals=0),
    )(near, weight)


def exchange(copies, axis, groups):
    return lax.all_to_all(copies, axis, 0, 0, tiled=True, axis_index_groups=groups)


def on_device(tokens, in_weight, out_weight, decay_rates, residues, skip_gain):
    seq_count = lax.axis_size("seq")
    chan_count = lax.axis_size("chan")
    rows, chans = tokens.shape
    hops = chan_count // 2
    same_half = [list(range(z, chan_count, 2)) for z in range(2)]
    other_half = [(c, c ^ 1) for c in range(chan_count)]

    swapped = lax.ppermute(tokens, "chan", other_half)
    copies = spread(hold(tokens), swapped, hops)
    copies, late_weight = lax.optimization_barrier((copies, out_weight))
    half = lax.axis_index("chan") % 2
    stripes = late_weight.reshape(hops, 2, chans, out_weight.shape[1])
    own_weight = lax.dynamic_index_in_dim(stripes, half, 1, keepdims=False).reshape(hops * chans, -1)
    given = lax.dynamic_index_in_dim(stripes, 1 - half, 1, keepdims=False).reshape(hops * chans, -1)
    other_weight = lax.ppermute(given, "chan", other_half)
    power, impulse, chunk, small = tables(
        decay_rates, residues, skip_gain[None, :], in_weight, rows
    )
    block = exchange(copies, "chan", same_half)
    block, other_weight = lax.optimization_barrier((block, other_weight))
    query, product, carry, states = project(block, in_weight, power, small, seq_count)
    states = lax.all_to_all(states, "seq", 0, 0, tiled=True)
    copies = combine(decay_rates, states, query, product, carry, power, impulse, chunk, hops)
    near = exchange(copies, "chan", same_half)
    theirs = lax.ppermute(partial_output(near, other_weight, BF16), "chan", other_half)
    ours = partial_output(near, own_weight, F32)
    return (ours + theirs.astype(F32)).astype(BF16)


def solution(mesh):
    return jax.shard_map(
        on_device,
        mesh=mesh,
        in_specs=(
            P("seq", "chan"),
            P(None, None, "chan"),
            P(None, "chan"),
            P(None, "chan"),
            P(None, "chan"),
            P("chan"),
        ),
        out_specs=P("seq", "chan"),
        check_vma=False,
    )
```
